32 devices in a mesh: seq: 8 (over z, x), tp: 4 (over y, core).
Axes of the slice: x: 2, y: 2, z: 4, core: 2. Of those that a mesh axis runs over, the one named last changes fastest.
Arguments:
- tokens: bfloat16 [4096, 4096], P(('seq', 'tp')), may hold values from -64 to 64, as said below
- joined_projection_weight: bfloat16 [4096, 6144], P(None, 'tp'), may hold values from -0.09375 to 0.09375
- adapter_down_weight: bfloat16 [4096, 64], replicated, may hold values from -0.09375 to 0.09375
- adapter_up_weight: bfloat16 [64, 6144], P(None, 'tp'), may hold values from -0.75 to 0.75
- document_index: int32 [4096], replicated, may hold values from 0 to 3, as said below
- query_to_key_head: int32 [32], replicated, may hold values from 0 to 7, as said below
Outputs:
- context: bfloat16 [4096, 4096], P(('seq', 'tp'))
The draws below stay inside these ranges and needn't reach their ends.
Inputs may be any that keep to these rules, and one draw needn't show every extreme that they name: `tokens`: rows of order one, except in the hidden draw where some rows have larger scales. `query_to_key_head`: each of 0 to 7 is named by exactly 4 query heads. `document_index`: never falling, starting at 0; each of the 4 documents covers 4096 / 16 or more positions.
All inputs are finite; a program needn't handle non-finite values.
Results may differ from the reference program's by a relative error of at most 0.012.
The reference program's roundings to bfloat16 on the way count: a program that leaves them out, or rounds other values in their place, can miss the bound.
Values may be sent and summed in bfloat16 or wider, within the bound.
A program may use at most 128 MiB of HBM per device.

```python
import jax
import jax.numpy as jnp
from jax import lax

MODEL_WIDTH = 4096
H = 32
KV = 8
DH = 128
ADAPTER_RANK = 64
DOCS = 4
S = 4096
JOINED_COLUMNS = 6144
N_TP = 4


def draw_tokens(key, part):
    noise_key = jax.random.fold_in(key, 0)
    drawn = jax.random.normal(noise_key, (S, MODEL_WIDTH), jnp.float32)
    return jnp.clip(drawn, -64.0, 64.0).astype(jnp.bfloat16)


def draw_document_index(key, part):
    length_key = jax.random.fold_in(key, 7)
    lengths = jax.random.randint(length_key, (DOCS - 1,), S // 16, 5 * S // 16, dtype=jnp.int32)
    bounds = jnp.cumsum(lengths).astype(jnp.int32)
    places = jnp.arange(S, dtype=jnp.int32)
    return jnp.sum((places[:, None] >= bounds[None, :]).astype(jnp.int32), axis=1).astype(jnp.int32)


def draw_query_to_key_head(key, part):
    order = jax.random.permutation(key, H)
    return (order % KV).astype(jnp.int32)


def level_of(rng, extent, shards, least, largest):
    level, own = 1.0, jax.random.fold_in(rng, 6)
    for dim, blocks in shards:
        heights = jnp.exp(jax.random.uniform(jax.random.fold_in(own, dim), (blocks,), jnp.float32, least / len(shards), largest / len(shards)))
        level = level * jnp.repeat(heights, extent[dim] // blocks).reshape([-1 if axis == dim else 1 for axis in range(len(extent))])
    return level


def gaussian(key, dims, spread, limit, shards=(), kind=jnp.bfloat16):
    gain = level_of(key, dims, shards, -0.22, 0.18) if shards else 1.0
    result = jax.random.normal(key, dims, jnp.float32) * spread * gain
    return jnp.minimum(jnp.maximum(result, -limit), limit).astype(kind)


def setup_inputs(seed: int = 0) -> dict:
    splits = jax.random.split(jax.random.key(seed), 7)
    return {
        "tokens": draw_tokens(jax.random.fold_in(splits[6], 71), 0),
        "joined_projection_weight": gaussian(splits[1], (MODEL_WIDTH, JOINED_COLUMNS), MODEL_WIDTH ** -0.5, 0.09375, ((1, 4),)),
        "adapter_down_weight": gaussian(splits[2], (MODEL_WIDTH, ADAPTER_RANK), MODEL_WIDTH ** -0.5, 0.09375),
        "adapter_up_weight": gaussian(splits[3], (ADAPTER_RANK, JOINED_COLUMNS), ADAPTER_RANK ** -0.5, 0.75, ((1, 4),)),
        "document_index": draw_document_index(jax.random.fold_in(splits[6], 71), 0),
        "query_to_key_head": draw_query_to_key_head(jax.random.fold_in(splits[6], 71), 0),
    }


ADAPTER_SCALE = 0.5
THETA = 500000.0


def rotate(values, places):
    half_dim = values.shape[-1] // 2
    frequency = THETA ** (-(jnp.arange(half_dim, dtype=jnp.float32) * 2.0) / values.shape[-1])
    angles = places[:, None] * frequency[None, :]
    cosine = jnp.cos(angles)[:, None, :]
    sine_part = jnp.sin(angles)[:, None, :]
    front_half = values[..., :half_dim]
    back_half = values[..., half_dim:]
    return jnp.concatenate([front_half * cosine - back_half * sine_part, back_half * cosine + front_half * sine_part], axis=-1)


def reference(tokens, joined_projection_weight, adapter_down_weight, adapter_up_weight, document_index, query_to_key_head):
    projected_rows = jnp.dot(tokens, joined_projection_weight, preferred_element_type=jnp.float32)
    adapter_middle = jnp.dot(tokens, adapter_down_weight, preferred_element_type=jnp.float32).astype(jnp.bfloat16)
    joined_output = projected_rows + ADAPTER_SCALE * jnp.dot(adapter_middle, adapter_up_weight, preferred_element_type=jnp.float32)
    query_group = H // N_TP
    key_group = KV // N_TP
    grouped = joined_output.reshape(S, N_TP, (query_group + 2 * key_group) * DH)
    queries = grouped[:, :, :query_group * DH].reshape(S, H, DH)
    keys = grouped[:, :, query_group * DH:(query_group + key_group) * DH].reshape(S, KV, DH)
    values = grouped[:, :, (query_group + key_group) * DH:].reshape(S, KV, DH)
    places = jnp.arange(S, dtype=jnp.int32).astype(jnp.float32)
    q_rot = rotate(queries, places).astype(jnp.bfloat16)
    k_rot = rotate(keys, places).astype(jnp.bfloat16)
    v_half = values.astype(jnp.bfloat16)
    k_head = k_rot[:, query_to_key_head]
    v_head = v_half[:, query_to_key_head]
    scale = DH ** -0.5
    query_block = min(1024, S)
    key_places = jnp.arange(S, dtype=jnp.int32)

    def head_out(head_index):
        q_one = lax.dynamic_index_in_dim(q_rot, head_index, 1, keepdims=False)
        k_one = lax.dynamic_index_in_dim(k_head, head_index, 1, keepdims=False)
        v_one = lax.dynamic_index_in_dim(v_head, head_index, 1, keepdims=False)

        def block_out(block_index):
            start = (block_index * query_block).astype(jnp.int32)
            q_tile = lax.dynamic_slice_in_dim(q_one, start, query_block, 0)
            tile_places = start + jnp.arange(query_block, dtype=jnp.int32)
            tile_segments = lax.dynamic_slice_in_dim(document_index, start, query_block, 0)
            scores = jnp.dot(q_tile, k_one.T, preferred_element_type=jnp.float32) * scale
            allowed = (key_places[None, :] <= tile_places[:, None]) & (document_index[None, :] == tile_segments[:, None])
            scores = jnp.where(allowed, scores, -jnp.inf)
            row_max = jnp.max(scores, axis=-1, keepdims=True)
            powers = jnp.exp(scores - row_max)
            weights = powers.astype(jnp.bfloat16)
            numer = jnp.dot(weights, v_one, preferred_element_type=jnp.float32)
            return (numer / jnp.sum(powers, axis=-1, keepdims=True)).astype(jnp.bfloat16)

        return lax.map(block_out, jnp.arange(S // query_block, dtype=jnp.int32)).reshape(S, DH)

    per_head = lax.map(head_out, jnp.arange(H, dtype=jnp.int32))
    return jnp.transpose(per_head, (1, 0, 2)).reshape(S, H * DH)
```

```python
import functools

import jax
import jax.numpy as jnp
from jax import lax
from jax.experimental import pallas as pl
from jax.experimental.pallas import tpu as pltpu
from jax.sharding import PartitionSpec as P

H = 32
KV = 8
DH = 128
GROUP = H // KV

ADAPTER_SCALE = 0.5
THETA = 500000.0
NEG_BIG = -1e30
LOG2_E = 1.4426950408889634


def rope_tables(places):
    half = DH // 2
    frequency = THETA ** (-(jnp.arange(half, dtype=jnp.float32) * 2.0) / DH)
    angles = places[:, None] * frequency[None, :]
    cosine, sine = jnp.cos(angles), jnp.sin(angles)
    return jnp.concatenate([cosine, cosine], 1), jnp.concatenate([-sine, sine], 1)


MESH = pl.DeviceIdType.MESH


def front_kernel(
    rotated_pairs, here, index_ref, tokens_ref, w_ref, down_ref, up_ref, cos_ref, sin_ref,
    q_ref, kv_ref,
    x_all, w_all, stage, landed_low, landed_high, sent, mid_ref,
    w_sem, local_sem, send_sem, x_sem, land_sem, q_sem, kv_sem, spread_sem,
):
    tp = lax.axis_index("tp")
    seq = lax.axis_index("seq")
    chips, _, own, _ = x_all.shape
    halves, half = 2, own // 2
    tp_count, seq_count = 2 * chips, q_ref.shape[0]
    steps = w_all.shape[0]
    wide = w_all.shape[2]
    pair = wide // DH
    chip, core = tp // 2, tp % 2
    partner = chip * 2 + (1 - core)
    landed = (landed_low, landed_high)
    sends = []

    def send(src, dst, sem, axis, target):
        copy = pltpu.make_async_remote_copy(
            src_ref=src, dst_ref=dst, send_sem=send_sem.at[len(sends)], recv_sem=sem,
            device_id={axis: target}, device_id_type=MESH,
        )
        copy.start()
        sends.append(copy)

    def arrived(dst, sem, axis, source):
        pltpu.make_async_remote_copy(
            src_ref=dst, dst_ref=dst, send_sem=send_sem.at[0], recv_sem=sem,
            device_id={axis: source}, device_id_type=MESH,
        ).wait_recv()

    def weight_copy(step):
        return pltpu.make_async_copy(
            w_ref.at[:, pl.ds(pl.multiple_of(step * wide, wide), wide)], w_all.at[step], w_sem.at[step]
        )

    own_copy = pltpu.make_async_copy(tokens_ref, x_all.at[chip, core], local_sem.at[0])
    own_copy.start()
    for step in range(steps):
        weight_copy(step).start()

    barrier = pltpu.get_barrier_semaphore()
    for k in range(1, tp_count):
        pl.semaphore_signal(
            barrier, inc=1, device_id={"tp": (tp + k) % tp_count}, device_id_type=MESH
        )
    for k in range(1, seq_count):
        pl.semaphore_signal(
            barrier, inc=1, device_id={"seq": (seq + k) % seq_count}, device_id_type=MESH
        )
    pl.semaphore_wait(barrier, tp_count - 1 + seq_count - 1)

    def rows_of(h):
        return pl.ds(h * half, half)

    others = [(chip + k) % chips for k in range(1, chips)]
    for h in range(halves):
        for other in others:
            send(
                tokens_ref.at[rows_of(h)], x_all.at[chip, core, rows_of(h)],
                x_sem.at[chip, core, h], "tp", other * 2 + core,
            )
        send(
            tokens_ref.at[rows_of(h)], x_all.at[chip, core, rows_of(h)],
            x_sem.at[chip, core, h], "tp", partner,
        )

    def compute(where, low, count, first):
        rows = pl.ds(low, count)
        x = x_all[where, :, rows, :].reshape(2 * count, x_all.shape[3])
        mid_ref[pl.ds(0, 2 * count)] = lax.dot_general(
            x, down_ref[...], (((1,), (1,)), ((), ())), preferred_element_type=jnp.float32
        ).astype(jnp.bfloat16)

        @pl.loop(0, steps)
        def _(step):
            if first:
                weight_copy(step).wait()
            x = x_all[where, :, rows, :].reshape(2 * count, x_all.shape[3])
            joined = jnp.dot(x, w_all[step], preferred_element_type=jnp.float32)
            joined = joined + ADAPTER_SCALE * jnp.dot(
                mid_ref[pl.ds(0, 2 * count)], up_ref[:, pl.ds(pl.multiple_of(step * wide, wide), wide)],
                preferred_element_type=jnp.float32
            )
            kind = step // rotated_pairs
            cosine = cos_ref[kind, where, :, rows, :].reshape(2 * count, DH)
            sine = sin_ref[kind, where, :, rows, :].reshape(2 * count, DH)
            for head in range(pair):
                part = joined[:, head * DH : (head + 1) * DH]
                part = part * cosine + pltpu.roll(part, DH // 2, 1) * sine
                part = part.astype(jnp.bfloat16)
                for k in range(2):
                    stage[where, k, step * pair + head, rows] = part[k * count : (k + 1) * count]

    def give(where, k, h, target):
        send(
            stage.at[where, k, :, rows_of(h)], landed[h].at[tp],
            land_sem.at[tp, h], "tp", target,
        )

    own_copy.wait()
    for h in range(halves):
        arrived(x_all.at[chip, 1 - core, rows_of(h)], x_sem.at[chip, 1 - core, h], "tp", partner)
    compute(chip, 0, own, True)
    keeps = [
        pltpu.make_async_copy(
            stage.at[chip, core, :, rows_of(h)], landed[h].at[tp], local_sem.at[5 * h]
        )
        for h in range(halves)
    ]
    for keep in keeps:
        keep.start()
    for h in range(halves):
        give(chip, 1 - core, h, partner)
    for h in range(halves):
        for other in others:
            block = x_all.at[other, core, rows_of(h)]
            arrived(block, x_sem.at[other, core, h], "tp", other * 2 + core)
            send(block, block, x_sem.at[other, core, h], "tp", partner)
        for other in others:
            arrived(
                x_all.at[other, 1 - core, rows_of(h)], x_sem.at[other, 1 - core, h], "tp", partner
            )
            compute(other, h * half, half, False)
            for k in range(2):
                give(other, k, h, other * 2 + k)
    for keep in keeps:
        keep.wait()
    q_per = H // tp_count
    kv_per = KV // tp_count
    near = [(seq + k) % seq_count for k in range(1, seq_count)]
    mine = []

    def hold(src, dst):
        copy = pltpu.make_async_copy(src, dst, local_sem.at[1 + len(mine)])
        copy.start()
        mine.append(copy)

    for h in range(halves):
        rows = rows_of(h)
        for k in range(1, tp_count):
            source = (tp + k) % tp_count
            arrived(landed[h].at[source], land_sem.at[source, h], "tp", source)

        @pl.loop(0, seq_count)
        def _(j):
            kv_head = j * here // GROUP
            for k in range(2):
                sent[j, here + k, rows] = landed[h][
                    kv_head // kv_per, q_per + k * kv_per + kv_head % kv_per
                ]

        for j in near:
            send(
                sent.at[j, pl.ds(here, 2), rows], kv_ref.at[tp, seq, :, rows],
                kv_sem.at[seq, h], "seq", j,
            )

        @pl.loop(0, seq_count)
        def _(j):
            for k in range(here):
                head = index_ref[j * here + k]
                sent[j, k, rows] = landed[h][head // q_per, head % q_per]

        for j in near:
            send(
                sent.at[j, pl.ds(0, here), rows], q_ref.at[seq, :, rows],
                q_sem.at[seq, h], "seq", j,
            )
        hold(sent.at[seq, pl.ds(here, 2), rows], kv_ref.at[tp, seq, :, rows])
        hold(sent.at[seq, pl.ds(0, here), rows], q_ref.at[seq, :, rows])

    for copy in mine:
        copy.wait()
    for h in range(halves):
        for n, source in enumerate([seq] + near[::-1]):
            block = kv_ref.at[tp, source, :, rows_of(h)]
            if n:
                arrived(block, kv_sem.at[source, h], "seq", source)
            for other in others:
                send(block, block, spread_sem.at[tp, source, h], "tp", other * 2 + core)
            send(block, block, spread_sem.at[tp, source, h], "tp", partner)
    for h in range(halves):
        for source in [seq] + near[::-1]:
            for other in others:
                far = other * 2 + core
                block = kv_ref.at[far, source, :, rows_of(h)]
                arrived(block, spread_sem.at[far, source, h], "tp", far)
                send(block, block, spread_sem.at[far, source, h], "tp", partner)
    for h in range(halves):
        for source in near:
            arrived(q_ref.at[source, :, rows_of(h)], q_sem.at[source, h], "seq", source)
        for k in range(chips):
            source = (chip + k) % chips * 2 + 1 - core
            for n in range(seq_count):
                arrived(
                    kv_ref.at[source, n, :, rows_of(h)], spread_sem.at[source, n, h], "tp", partner
                )
    for copy in sends:
        copy.wait_send()


def front(index, tokens, w, down, up, cosine, sine, tp_count, seq_count, rotated_heads):
    own, width = tokens.shape
    heads = w.shape[1] // DH
    pair = 2
    steps = heads // pair
    chips = tp_count // 2
    here = H // seq_count
    rank = down.shape[1]
    vmem = pl.BlockSpec(memory_space=pltpu.VMEM)
    anywhere = pl.BlockSpec(memory_space=pl.ANY)
    count = (
        2 * chips + 2 + 2 * (chips - 1) * 4 + 4 * (seq_count - 1) + 2 * seq_count * (tp_count - 1)
    )
    bf16 = jnp.bfloat16
    return pl.pallas_call(
        functools.partial(front_kernel, rotated_heads // pair, here),
        in_specs=[pl.BlockSpec(memory_space=pltpu.SMEM), anywhere, anywhere, vmem, vmem, vmem, vmem],
        out_specs=[anywhere, anywhere],
        out_shape=[
            jax.ShapeDtypeStruct((seq_count, here, own, DH), bf16),
            jax.ShapeDtypeStruct((tp_count, seq_count, 2, own, DH), bf16),
        ],
        scratch_shapes=[
            pltpu.VMEM((chips, 2, own, width), bf16),
            pltpu.VMEM((steps, width, pair * DH), bf16),
            pltpu.VMEM((chips, 2, heads, own, DH), bf16),
            pltpu.VMEM((tp_count, heads, own // 2, DH), bf16),
            pltpu.VMEM((tp_count, heads, own // 2, DH), bf16),
            pltpu.VMEM((seq_count, here + 2, own, DH), bf16),
            pltpu.VMEM((2 * own, rank), bf16),
            pltpu.SemaphoreType.DMA((steps,)),
            pltpu.SemaphoreType.DMA((6,)),
            pltpu.SemaphoreType.DMA((count,)),
            pltpu.SemaphoreType.DMA((chips, 2, 2)),
            pltpu.SemaphoreType.DMA((tp_count, 2)),
            pltpu.SemaphoreType.DMA((seq_count, 2)),
            pltpu.SemaphoreType.DMA((seq_count, 2)),
            pltpu.SemaphoreType.DMA((tp_count, seq_count, 2)),
        ],
        compiler_params=pltpu.CompilerParams(collective_id=0, has_side_effects=True),
        name="front",
    )(index, tokens, w, down.T, up, cosine, sine)


def finish_kernel(slot_ref, in_ref, out_ref, landed, send_sem, land_sem, local_sem):
    seq = lax.axis_index("seq")
    seq_count, here, _, _ = landed.shape
    own_copy = pltpu.make_async_copy(in_ref.at[seq], landed.at[seq], local_sem.at[0])
    own_copy.start()
    near = [(seq + k) % seq_count for k in range(1, seq_count)]
    barrier = pltpu.get_barrier_semaphore()
    for j in near:
        pl.semaphore_signal(barrier, inc=1, device_id={"seq": j}, device_id_type=MESH)
    pl.semaphore_wait(barrier, seq_count - 1)
    sends = []
    for n, j in enumerate(near):
        copy = pltpu.make_async_remote_copy(
            src_ref=in_ref.at[j], dst_ref=landed.at[seq], send_sem=send_sem.at[n],
            recv_sem=land_sem.at[seq], device_id={"seq": j}, device_id_type=MESH,
        )
        copy.start()
        sends.append(copy)
    own_copy.wait()
    for j in near:
        pltpu.make_async_remote_copy(
            src_ref=landed.at[j], dst_ref=landed.at[j], send_sem=send_sem.at[0],
            recv_sem=land_sem.at[j], device_id={"seq": j}, device_id_type=MESH,
        ).wait_recv()
    for head in range(seq_count * here):
        slot = slot_ref[head]
        out_ref[:, head * DH : (head + 1) * DH] = landed[slot // here, slot % here]
    for copy in sends:
        copy.wait_send()


def finish(slot, context):
    seq_count, here, rows, _ = context.shape
    return pl.pallas_call(
        finish_kernel,
        in_specs=[pl.BlockSpec(memory_space=pltpu.SMEM), pl.BlockSpec(memory_space=pl.ANY)],
        out_specs=pl.BlockSpec(memory_space=pltpu.VMEM),
        out_shape=jax.ShapeDtypeStruct((rows, seq_count * here * DH), context.dtype),
        scratch_shapes=[
            pltpu.VMEM(context.shape, context.dtype),
            pltpu.SemaphoreType.DMA((seq_count,)),
            pltpu.SemaphoreType.DMA((seq_count,)),
            pltpu.SemaphoreType.DMA((1,)),
        ],
        compiler_params=pltpu.CompilerParams(collective_id=1, has_side_effects=True),
        name="finish",
    )(slot, context)


def attend_kernel(heads, scalar_ref, q_ref, kv_ref, doc_ref, out_ref):
    step = pl.program_id(0)
    tp = lax.axis_index("tp")
    chunks, _, _, own, _ = kv_ref.shape
    block = chunks * own
    rows = heads * own
    q = q_ref[0, :heads].reshape(rows, DH)
    place = step * block + tp * own
    first = jnp.sum((doc_ref[...] < scalar_ref[place]).astype(jnp.int32))
    docs = doc_ref[pl.ds(step * chunks + tp, 1), :]
    docs = jnp.broadcast_to(docs, (own, own)).T[:, :1]
    docs = jnp.concatenate([docs] * heads, 0)
    places = place + lax.broadcasted_iota(jnp.int32, (own, 1), 0)
    places = jnp.concatenate([places] * heads, 0)
    factor = (DH**-0.5) * LOG2_E

    def body(index, carry, own_block=False):
        top, total, acc = carry
        keys = kv_ref[:, index, 0].reshape(block, DH)
        values = kv_ref[:, index, 1].reshape(block, DH)
        scores = lax.dot_general(
            q, keys, (((1,), (1,)), ((), ())), preferred_element_type=jnp.float32
        )
        at = index * block + lax.broadcasted_iota(jnp.int32, (1, block), 1)
        key_docs = jnp.concatenate(
            [doc_ref[pl.ds(index * chunks + c, 1), :] for c in range(chunks)], 1
        )
        kept = key_docs == docs
        if own_block:
            kept = kept & (at <= places)
        scores = jnp.where(kept, scores, NEG_BIG)
        new_top = jnp.maximum(top, jnp.max(scores, 1, keepdims=True))
        shrink = jnp.exp2((top - new_top) * factor)
        powers = jnp.exp2((scores - new_top) * factor)
        total = total * shrink + jnp.sum(powers, 1, keepdims=True)
        acc = acc * shrink + jnp.dot(
            powers.astype(jnp.bfloat16), values, preferred_element_type=jnp.float32
        )
        return new_top, total, acc

    last = place // block
    start = (
        jnp.full((rows, 1), NEG_BIG, jnp.float32),
        jnp.zeros((rows, 1), jnp.float32),
        jnp.zeros((rows, DH), jnp.float32),
    )
    carry = body(last, start, True)
    top, total, acc = lax.fori_loop(first // block, last, body, carry)
    out_ref[0] = (acc / total).astype(jnp.bfloat16).reshape(heads, own, DH)


def attend(document_index, q, kv, heads):
    steps, slabs, own, _ = q.shape
    return pl.pallas_call(
        functools.partial(attend_kernel, heads),
        grid_spec=pltpu.PrefetchScalarGridSpec(
            num_scalar_prefetch=1,
            grid=(steps,),
            in_specs=[
                pl.BlockSpec((1, slabs, own, DH), lambda i, *_: (i, 0, 0, 0)),
                pl.BlockSpec(kv.shape, lambda i, *_: (0,) * 5),
                pl.BlockSpec((steps * kv.shape[0], own), lambda i, *_: (0, 0)),
            ],
            out_specs=pl.BlockSpec((1, heads, own, DH), lambda i, *_: (i, 0, 0, 0)),
        ),
        out_shape=jax.ShapeDtypeStruct((steps, heads, own, DH), jnp.bfloat16),
        name="attend",
    )(document_index, q, kv, document_index.reshape(-1, own))


def head_tables(query_to_key_head):
    heads = jnp.arange(H, dtype=jnp.int32)
    same = query_to_key_head[:, None] == query_to_key_head[None, :]
    earlier = heads[None, :] < heads[:, None]
    slot = GROUP * query_to_key_head + jnp.sum((same & earlier).astype(jnp.int32), 1)
    order = jnp.sum(jnp.where(slot[None, :] == heads[:, None], heads[None, :], 0), 1)
    return order.astype(jnp.int32), slot.astype(jnp.int32)


def per_device(
    tokens,
    joined_projection_weight,
    adapter_down_weight,
    adapter_up_weight,
    document_index,
    query_to_key_head,
):
    tp_count = lax.axis_size("tp")
    seq_count = lax.axis_size("seq")
    tp_rank = lax.axis_index("tp")
    seq_rank = lax.axis_index("seq")
    own = tokens.shape[0]
    block = own * tp_count
    here = H // seq_count
    q_per, kv_per = H // tp_count, KV // tp_count

    index, slot = head_tables(query_to_key_head)
    places = (seq_rank * block + jnp.arange(block, dtype=jnp.int32)).astype(jnp.float32)
    cosine, sine = rope_tables(places)
    table = (1, tp_count // 2, 2, own, DH)
    cosine = jnp.concatenate([cosine.reshape(table), jnp.ones(table, jnp.float32)])
    sine = jnp.concatenate([sine.reshape(table), jnp.zeros(table, jnp.float32)])
    held, kv = front(
        index, tokens, joined_projection_weight, adapter_down_weight, adapter_up_weight,
        cosine, sine, tp_count, seq_count, q_per + kv_per,
    )
    context = attend(document_index, held, kv, here)
    return finish(slot, context)


def solution(mesh):
    return jax.shard_map(
        per_device,
        mesh=mesh,
        in_specs=(P(("seq", "tp"), None), P(None, "tp"), P(), P(None, "tp"), P(), P()),
        out_specs=P(("seq", "tp"), None),
        check_vma=False,
    )
```

```python
import functools

import jax
import jax.numpy as jnp
from jax import lax
from jax.experimental import pallas as pl
from jax.experimental.pallas import tpu as pltpu
from jax.sharding import PartitionSpec as P

H = 32
KV = 8
DH = 128
GROUP = H // KV

ADAPTER_SCALE = 0.5
THETA = 500000.0
NEG_BIG = -1e30
LOG2_E = 1.4426950408889634


def rope_tables(places):
    half = DH // 2
    frequency = THETA ** (-(jnp.arange(half, dtype=jnp.float32) * 2.0) / DH)
    angles = places[:, None] * frequency[None, :]
    cosine, sine = jnp.cos(angles), jnp.sin(angles)
    return jnp.concatenate([cosine, cosine], 1), jnp.concatenate([-sine, sine], 1)


MESH = pl.DeviceIdType.MESH


def front_kernel(
    rotated_pairs, here, ahead, index_ref, tokens_ref, w_ref, down_ref, up_ref, cos_ref, sin_ref,
    q_ref, kv_ref,
    x_all, w_all, stage, sent, mid_ref,
    w_sem, own_sem, keep_sem, hold_sem, send_sem, x_sem, land_sem, q_sem, kv_sem, spread_sem,
    *landed,
):
    tp = lax.axis_index("tp")
    seq = lax.axis_index("seq")
    chips, _, own, width = x_all.shape
    parts, part = len(landed), landed[0].shape[2]
    tp_count, seq_count = 2 * chips, q_ref.shape[0]
    steps = w_all.shape[0]
    wide = w_all.shape[2]
    pair = wide // DH
    chip, core = tp // 2, tp % 2
    partner = chip * 2 + (1 - core)
    others = [(chip + k) % chips for k in range(1, chips)]
    near = [(seq + k) % seq_count for k in range(1, seq_count)]
    q_per = H // tp_count
    kv_per = KV // tp_count
    sends = []
    locals_ = []

    def send(src, dst, sem, axis, target):
        copy = pltpu.make_async_remote_copy(
            src_ref=src, dst_ref=dst, send_sem=send_sem.at[len(sends)], recv_sem=sem,
            device_id={axis: target}, device_id_type=MESH,
        )
        copy.start()
        sends.append(copy)

    def arrived(dst, sem, axis, source):
        pltpu.make_async_remote_copy(
            src_ref=dst, dst_ref=dst, send_sem=send_sem.at[0], recv_sem=sem,
            device_id={axis: source}, device_id_type=MESH,
        ).wait_recv()

    def weight_copy(step):
        return pltpu.make_async_copy(
            w_ref.at[:, pl.ds(pl.multiple_of(step * wide, wide), wide)], w_all.at[step], w_sem.at[step]
        )

    def rows_of(c):
        return pl.ds(c * part, part)

    own_copy = pltpu.make_async_copy(tokens_ref, x_all.at[chip, core], own_sem)
    own_copy.start()
    for step in range(steps):
        weight_copy(step).start()

    barrier = pltpu.get_barrier_semaphore()
    for k in range(1, tp_count):
        pl.semaphore_signal(
            barrier, inc=1, device_id={"tp": (tp + k) % tp_count}, device_id_type=MESH
        )
    for k in range(1, seq_count):
        pl.semaphore_signal(
            barrier, inc=1, device_id={"seq": (seq + k) % seq_count}, device_id_type=MESH
        )
    pl.semaphore_wait(barrier, tp_count - 1 + seq_count - 1)

    def send_tokens(c):
        for other in others:
            send(
                tokens_ref.at[rows_of(c)], x_all.at[chip, core, rows_of(c)],
                x_sem.at[chip, core, c], "tp", other * 2 + core,
            )

    for c in range(min(ahead, parts)):
        send_tokens(c)
    for c in range(parts):
        send(
            tokens_ref.at[rows_of(c)], x_all.at[chip, core, rows_of(c)],
            x_sem.at[chip, core, c], "tp", partner,
        )

    def compute(where, low, count, first):
        rows = pl.ds(low, count)
        x = x_all[where, :, rows, :].reshape(2 * count, width)
        mid_ref[pl.ds(0, 2 * count)] = lax.dot_general(
            x, down_ref[...], (((1,), (1,)), ((), ())), preferred_element_type=jnp.float32
        ).astype(jnp.bfloat16)

        @pl.loop(0, steps)
        def _(step):
            if first:
                weight_copy(step).wait()
            x = x_all[where, :, rows, :].reshape(2 * count, width)
            joined = jnp.dot(x, w_all[step], preferred_element_type=jnp.float32)
            joined = joined + ADAPTER_SCALE * jnp.dot(
                mid_ref[pl.ds(0, 2 * count)], up_ref[:, pl.ds(pl.multiple_of(step * wide, wide), wide)],
                preferred_element_type=jnp.float32
            )
            kind = step // rotated_pairs
            cosine = cos_ref[kind, where, :, rows, :].reshape(2 * count, DH)
            sine = sin_ref[kind, where, :, rows, :].reshape(2 * count, DH)
            for head in range(pair):
                piece = joined[:, head * DH : (head + 1) * DH]
                piece = piece * cosine + pltpu.roll(piece, DH // 2, 1) * sine
                piece = piece.astype(jnp.bfloat16)
                for k in range(2):
                    stage[where, k, step * pair + head, rows] = piece[k * count : (k + 1) * count]

    def give(where, k, c, target):
        send(
            stage.at[where, k, :, rows_of(c)], landed[c].at[tp], land_sem.at[tp, c], "tp", target
        )

    def hold(src, dst, sem):
        copy = pltpu.make_async_copy(src, dst, sem)
        copy.start()
        locals_.append(copy)

    def project(c):
        for other in others:
            block = x_all.at[other, core, rows_of(c)]
            arrived(block, x_sem.at[other, core, c], "tp", other * 2 + core)
            send(block, block, x_sem.at[other, core, c], "tp", partner)
        for other in others:
            arrived(
                x_all.at[other, 1 - core, rows_of(c)], x_sem.at[other, 1 - core, c], "tp", partner
            )
            compute(other, c * part, part, False)
            for k in range(2):
                give(other, k, c, other * 2 + k)
        if c + ahead < parts:
            send_tokens(c + ahead)

    def exchange(c):
        rows = rows_of(c)
        keeps[c].wait()
        for k in range(1, tp_count):
            source = (tp + k) % tp_count
            arrived(landed[c].at[source], land_sem.at[source, c], "tp", source)

        @pl.loop(0, seq_count)
        def _(j):
            kv_head = j * here // GROUP
            for k in range(2):
                sent[j, here + k, rows] = landed[c][
                    kv_head // kv_per, q_per + k * kv_per + kv_head % kv_per
                ]

        for j in near:
            send(
                sent.at[j, pl.ds(here, 2), rows], kv_ref.at[tp, seq, :, rows],
                kv_sem.at[seq, c], "seq", j,
            )
        hold(sent.at[seq, pl.ds(here, 2), rows], kv_ref.at[tp, seq, :, rows], hold_sem.at[0, c])

        @pl.loop(0, seq_count)
        def _(j):
            for k in range(here):
                head = index_ref[j * here + k]
                sent[j, k, rows] = landed[c][head // q_per, head % q_per]

        for j in near:
            send(
                sent.at[j, pl.ds(0, here), rows], q_ref.at[seq, :, rows],
                q_sem.at[seq, c], "seq", j,
            )
        hold(sent.at[seq, pl.ds(0, here), rows], q_ref.at[seq, :, rows], hold_sem.at[1, c])

    def spread(c):
        rows = rows_of(c)
        locals_[2 * c].wait()
        for source in near:
            arrived(kv_ref.at[tp, source, :, rows], kv_sem.at[source, c], "seq", source)
        block = kv_ref.at[tp, :, :, rows]
        for other in others:
            send(block, block, spread_sem.at[tp, c], "tp", other * 2 + core)
        send(block, block, spread_sem.at[tp, c], "tp", partner)

    def forward(c):
        for other in others:
            far = other * 2 + core
            block = kv_ref.at[far, :, :, rows_of(c)]
            arrived(block, spread_sem.at[far, c], "tp", far)
            send(block, block, spread_sem.at[far, c], "tp", partner)

    own_copy.wait()
    for c in range(parts):
        arrived(x_all.at[chip, 1 - core, rows_of(c)], x_sem.at[chip, 1 - core, c], "tp", partner)
    compute(chip, 0, own, True)
    keeps = [
        pltpu.make_async_copy(
            stage.at[chip, core, :, rows_of(c)], landed[c].at[tp], keep_sem.at[c]
        )
        for c in range(parts)
    ]
    for c in range(parts):
        keeps[c].start()
        give(chip, 1 - core, c, partner)

    for step in range(parts + 3):
        if step < parts:
            project(step)
        if 0 <= step - 1 < parts:
            exchange(step - 1)
        if 0 <= step - 2 < parts:
            spread(step - 2)
        if 0 <= step - 3 < parts:
            forward(step - 3)

    for c in range(parts):
        rows = rows_of(c)
        locals_[2 * c + 1].wait()
        for source in near:
            arrived(q_ref.at[source, :, rows], q_sem.at[source, c], "seq", source)
        for k in range(chips):
            source = (chip + k) % chips * 2 + 1 - core
            arrived(kv_ref.at[source, :, :, rows], spread_sem.at[source, c], "tp", partner)
    for copy in sends:
        copy.wait_send()


PARTS = 4
AHEAD = 2


def front(index, tokens, w, down, up, cosine, sine, tp_count, seq_count, rotated_heads):
    own, width = tokens.shape
    heads = w.shape[1] // DH
    pair = 2
    steps = heads // pair
    chips = tp_count // 2
    here = H // seq_count
    rank = down.shape[1]
    parts = PARTS
    vmem = pl.BlockSpec(memory_space=pltpu.VMEM)
    anywhere = pl.BlockSpec(memory_space=pl.ANY)
    tokens_out = parts * (2 * (chips - 1) + 1)
    results_out = parts * (2 * (chips - 1) + 1)
    spread_out = parts * (2 * (chips - 1) + 1)
    count = tokens_out + results_out + spread_out + 2 * parts * (seq_count - 1)
    bf16 = jnp.bfloat16
    dma = pltpu.SemaphoreType.DMA
    return pl.pallas_call(
        functools.partial(front_kernel, rotated_heads // pair, here, AHEAD),
        in_specs=[pl.BlockSpec(memory_space=pltpu.SMEM), anywhere, anywhere, vmem, vmem, vmem, vmem],
        out_specs=[anywhere, anywhere],
        out_shape=[
            jax.ShapeDtypeStruct((seq_count, here, own, DH), bf16),
            jax.ShapeDtypeStruct((tp_count, seq_count, 2, own, DH), bf16),
        ],
        scratch_shapes=[
            pltpu.VMEM((chips, 2, own, width), bf16),
            pltpu.VMEM((steps, width, pair * DH), bf16),
            pltpu.VMEM((chips, 2, heads, own, DH), bf16),
            pltpu.VMEM((seq_count, here + 2, own, DH), bf16),
            pltpu.VMEM((2 * own, rank), bf16),
            dma((steps,)),
            dma(()),
            dma((parts,)),
            dma((2, parts)),
            dma((count,)),
            dma((chips, 2, parts)),
            dma((tp_count, parts)),
            dma((seq_count, parts)),
            dma((seq_count, parts)),
            dma((tp_count, parts)),
        ]
        + [pltpu.VMEM((tp_count, heads, own // parts, DH), bf16)] * parts,
        compiler_params=pltpu.CompilerParams(collective_id=0, has_side_effects=True),
        name="front",
    )(index, tokens, w, down.T, up, cosine, sine)


def tail_kernel(
    slot_ref, q_hbm, kv_hbm, doc_ref, out_ref,
    q_ref, kv_ref, context, landed, send_sem, land_sem, local_sem,
):
    tp = lax.axis_index("tp")
    seq = lax.axis_index("seq")
    seq_count, heads, own, _ = q_ref.shape
    chunks = kv_ref.shape[0]
    block = chunks * own
    rows = heads * own
    loads = [
        pltpu.make_async_copy(q_hbm, q_ref, local_sem.at[0]),
        pltpu.make_async_copy(kv_hbm, kv_ref, local_sem.at[1]),
    ]
    for load in loads:
        load.start()
    barrier = pltpu.get_barrier_semaphore()
    for k in range(1, seq_count):
        pl.semaphore_signal(
            barrier, inc=1, device_id={"seq": (seq + k) % seq_count}, device_id_type=MESH
        )
    pl.semaphore_wait(barrier, seq_count - 1)
    for load in loads:
        load.wait()
    factor = (DH**-0.5) * LOG2_E

    def toggled(change):
        result, bit = 0, 1
        while bit < seq_count:
            mine, flip = seq // bit % 2, change // bit % 2
            result = result + bit * (mine + flip - 2 * mine * flip)
            bit *= 2
        return result

    def attend(step):
        q = q_ref[step].reshape(rows, DH)
        docs = doc_ref[pl.ds(step * chunks + tp, 1), :]
        docs = jnp.broadcast_to(docs, (own, own)).T[:, :1]
        docs = jnp.concatenate([docs] * heads, 0)
        places = tp * own + lax.broadcasted_iota(jnp.int32, (own, 1), 0)
        places = jnp.concatenate([places] * heads, 0)

        def body(index, carry, own_block=False):
            top, total, acc = carry
            keys = kv_ref[:, index, 0].reshape(block, DH)
            values = kv_ref[:, index, 1].reshape(block, DH)
            scores = lax.dot_general(
                q, keys, (((1,), (1,)), ((), ())), preferred_element_type=jnp.float32
            )
            key_docs = jnp.concatenate(
                [doc_ref[pl.ds(index * chunks + c, 1), :] for c in range(chunks)], 1
            )
            kept = key_docs == docs
            if own_block:
                kept = kept & (lax.broadcasted_iota(jnp.int32, (1, block), 1) <= places)
            scores = jnp.where(kept, scores, NEG_BIG)
            new_top = jnp.maximum(top, jnp.max(scores, 1, keepdims=True))
            shrink = jnp.exp2((top - new_top) * factor)
            powers = jnp.exp2((scores - new_top) * factor)
            total = total * shrink + jnp.sum(powers, 1, keepdims=True)
            acc = acc * shrink + jnp.dot(
                powers.astype(jnp.bfloat16), values, preferred_element_type=jnp.float32
            )
            return new_top, total, acc

        start = (
            jnp.full((rows, 1), NEG_BIG, jnp.float32),
            jnp.zeros((rows, 1), jnp.float32),
            jnp.zeros((rows, DH), jnp.float32),
        )
        _, total, acc = lax.fori_loop(0, step, body, body(step, start, True))
        return (acc / total).astype(jnp.bfloat16).reshape(heads, own, DH)

    def outgoing(change):
        target = toggled(change)
        return target, pltpu.make_async_remote_copy(
            src_ref=context.at[change], dst_ref=landed.at[seq], send_sem=send_sem.at[change],
            recv_sem=land_sem.at[seq], device_id={"seq": target}, device_id_type=MESH,
        )

    def give(change):
        target, copy = outgoing(change)
        context[change] = attend(target)
        copy.start()

    half = seq_count // 2

    @pl.loop(0, half)
    def _(i):
        give(half + i)

    @pl.loop(0, half - 1)
    def _(i):
        give(half - 1 - i)

    landed[seq] = attend(seq)

    @pl.loop(1, seq_count)
    def _(change):
        source = toggled(change)
        pltpu.make_async_remote_copy(
            src_ref=landed.at[source], dst_ref=landed.at[source], send_sem=send_sem.at[0],
            recv_sem=land_sem.at[source], device_id={"seq": source}, device_id_type=MESH,
        ).wait_recv()

    for head in range(seq_count * heads):
        slot = slot_ref[head]
        out_ref[:, head * DH : (head + 1) * DH] = landed[slot // heads, slot % heads]

    @pl.loop(1, seq_count)
    def _(change):
        outgoing(change)[1].wait_send()


def tail(slot, q, kv, document_index):
    seq_count, heads, own, _ = q.shape
    vmem = pl.BlockSpec(memory_space=pltpu.VMEM)
    anywhere = pl.BlockSpec(memory_space=pl.ANY)
    return pl.pallas_call(
        tail_kernel,
        in_specs=[pl.BlockSpec(memory_space=pltpu.SMEM), anywhere, anywhere, vmem],
        out_specs=vmem,
        out_shape=jax.ShapeDtypeStruct((own, seq_count * heads * DH), q.dtype),
        scratch_shapes=[
            pltpu.VMEM(q.shape, q.dtype),
            pltpu.VMEM(kv.shape, kv.dtype),
            pltpu.VMEM(q.shape, q.dtype),
            pltpu.VMEM(q.shape, q.dtype),
            pltpu.SemaphoreType.DMA((seq_count,)),
            pltpu.SemaphoreType.DMA((seq_count,)),
            pltpu.SemaphoreType.DMA((2,)),
        ],
        compiler_params=pltpu.CompilerParams(collective_id=1, has_side_effects=True),
        name="tail",
    )(slot, q, kv, document_index.reshape(-1, own))


def head_tables(query_to_key_head):
    heads = jnp.arange(H, dtype=jnp.int32)
    same = query_to_key_head[:, None] == query_to_key_head[None, :]
    earlier = heads[None, :] < heads[:, None]
    slot = GROUP * query_to_key_head + jnp.sum((same & earlier).astype(jnp.int32), 1)
    order = jnp.sum(jnp.where(slot[None, :] == heads[:, None], heads[None, :], 0), 1)
    return order.astype(jnp.int32), slot.astype(jnp.int32)


def per_device(
    tokens,
    joined_projection_weight,
    adapter_down_weight,
    adapter_up_weight,
    document_index,
    query_to_key_head,
):
    tp_count = lax.axis_size("tp")
    seq_count = lax.axis_size("seq")
    tp_rank = lax.axis_index("tp")
    seq_rank = lax.axis_index("seq")
    own = tokens.shape[0]
    block = own * tp_count
    here = H // seq_count
    q_per, kv_per = H // tp_count, KV // tp_count

    index, slot = head_tables(query_to_key_head)
    places = (seq_rank * block + jnp.arange(block, dtype=jnp.int32)).astype(jnp.float32)
    cosine, sine = rope_tables(places)
    table = (1, tp_count // 2, 2, own, DH)
    cosine = jnp.concatenate([cosine.reshape(table), jnp.ones(table, jnp.float32)])
    sine = jnp.concatenate([sine.reshape(table), jnp.zeros(table, jnp.float32)])
    held, kv = front(
        index, tokens, joined_projection_weight, adapter_down_weight, adapter_up_weight,
        cosine, sine, tp_count, seq_count, q_per + kv_per,
    )
    return tail(slot, held, kv, document_index)


def solution(mesh):
    return jax.shard_map(
        per_device,
        mesh=mesh,
        in_specs=(P(("seq", "tp"), None), P(None, "tp"), P(), P(None, "tp"), P(), P()),
        out_specs=P(("seq", "tp"), None),
        check_vma=False,
    )
```

```python
import functools

import jax
import jax.numpy as jnp
from jax import lax
from jax.experimental import pallas as pl
from jax.experimental.pallas import tpu as pltpu
from jax.sharding import PartitionSpec as P

H = 32
KV = 8
DH = 128
GROUP = H // KV

ADAPTER_SCALE = 0.5
THETA = 500000.0
NEG_BIG = -1e30
LOG2_E = 1.4426950408889634


def rope_tables(places):
    half = DH // 2
    frequency = THETA ** (-(jnp.arange(half, dtype=jnp.float32) * 2.0) / DH)
    angles = places[:, None] * frequency[None, :]
    cosine, sine = jnp.cos(angles), jnp.sin(angles)
    return jnp.concatenate([cosine, cosine], 1), jnp.concatenate([-sine, sine], 1)


MESH = pl.DeviceIdType.MESH


def layer_kernel(
    rotated_pairs, here, ahead, index_ref, slot_ref, doc_ref,
    tokens_ref, w_ref, down_ref, up_ref, cos_ref, sin_ref, out_ref,
    x_all, w_all, stage, sent, mid_ref, q_ref, kv_ref, context, final,
    w_sem, own_sem, keep_sem, hold_sem, send_sem, x_sem, land_sem, q_sem, kv_sem, spread_sem,
    give_sem, final_sem, *landed,
):
    tp = lax.axis_index("tp")
    seq = lax.axis_index("seq")
    chips, _, own, width = x_all.shape
    parts, part = len(landed), landed[0].shape[2]
    tp_count, seq_count = 2 * chips, q_ref.shape[0]
    steps = w_all.shape[0]
    wide = w_all.shape[2]
    pair = wide // DH
    chip, core = tp // 2, tp % 2
    partner = chip * 2 + (1 - core)
    others = [(chip + k) % chips for k in range(1, chips)]
    near = [(seq + k) % seq_count for k in range(1, seq_count)]
    q_per = H // tp_count
    kv_per = KV // tp_count
    sends = []
    locals_ = []

    def send(src, dst, sem, axis, target):
        copy = pltpu.make_async_remote_copy(
            src_ref=src, dst_ref=dst, send_sem=send_sem.at[len(sends)], recv_sem=sem,
            device_id={axis: target}, device_id_type=MESH,
        )
        copy.start()
        sends.append(copy)

    def arrived(dst, sem, axis, source):
        pltpu.make_async_remote_copy(
            src_ref=dst, dst_ref=dst, send_sem=send_sem.at[0], recv_sem=sem,
            device_id={axis: source}, device_id_type=MESH,
        ).wait_recv()

    def weight_copy(step):
        return pltpu.make_async_copy(
            w_ref.at[:, pl.ds(pl.multiple_of(step * wide, wide), wide)], w_all.at[step], w_sem.at[step]
        )

    def rows_of(c):
        return pl.ds(c * part, part)

    own_copy = pltpu.make_async_copy(tokens_ref, x_all.at[chip, core], own_sem)
    own_copy.start()
    for step in range(steps):
        weight_copy(step).start()

    barrier = pltpu.get_barrier_semaphore()
    for k in range(1, tp_count):
        pl.semaphore_signal(
            barrier, inc=1, device_id={"tp": (tp + k) % tp_count}, device_id_type=MESH
        )
    for k in range(1, seq_count):
        pl.semaphore_signal(
            barrier, inc=1, device_id={"seq": (seq + k) % seq_count}, device_id_type=MESH
        )
    pl.semaphore_wait(barrier, tp_count - 1 + seq_count - 1)

    def send_tokens(c):
        for other in others:
            send(
                tokens_ref.at[rows_of(c)], x_all.at[chip, core, rows_of(c)],
                x_sem.at[chip, core, c], "tp", other * 2 + core,
            )

    for c in range(min(ahead, parts)):
        send_tokens(c)
    for c in range(parts):
        send(
            tokens_ref.at[rows_of(c)], x_all.at[chip, core, rows_of(c)],
            x_sem.at[chip, core, c], "tp", partner,
        )

    def compute(where, low, count, first):
        rows = pl.ds(low, count)
        x = x_all[where, :, rows, :].reshape(2 * count, width)
        mid_ref[pl.ds(0, 2 * count)] = lax.dot_general(
            x, down_ref[...], (((1,), (1,)), ((), ())), preferred_element_type=jnp.float32
        ).astype(jnp.bfloat16)

        @pl.loop(0, steps)
        def _(step):
            if first:
                weight_copy(step).wait()
            x = x_all[where, :, rows, :].reshape(2 * count, width)
            joined = jnp.dot(x, w_all[step], preferred_element_type=jnp.float32)
            joined = joined + ADAPTER_SCALE * jnp.dot(
                mid_ref[pl.ds(0, 2 * count)], up_ref[:, pl.ds(pl.multiple_of(step * wide, wide), wide)],
                preferred_element_type=jnp.float32
            )
            kind = step // rotated_pairs
            cosine = cos_ref[kind, where, :, rows, :].reshape(2 * count, DH)
            sine = sin_ref[kind, where, :, rows, :].reshape(2 * count, DH)
            for head in range(pair):
                piece = joined[:, head * DH : (head + 1) * DH]
                piece = piece * cosine + pltpu.roll(piece, DH // 2, 1) * sine
                piece = piece.astype(jnp.bfloat16)
                for k in range(2):
                    stage[where, k, step * pair + head, rows] = piece[k * count : (k + 1) * count]

    def give(where, k, c, target):
        send(
            stage.at[where, k, :, rows_of(c)], landed[c].at[tp], land_sem.at[tp, c], "tp", target
        )

    def hold(src, dst, sem):
        copy = pltpu.make_async_copy(src, dst, sem)
        copy.start()
        locals_.append(copy)

    def project(c):
        for other in others:
            block = x_all.at[other, core, rows_of(c)]
            arrived(block, x_sem.at[other, core, c], "tp", other * 2 + core)
            send(block, block, x_sem.at[other, core, c], "tp", partner)
        for other in others:
            arrived(
                x_all.at[other, 1 - core, rows_of(c)], x_sem.at[other, 1 - core, c], "tp", partner
            )
            compute(other, c * part, part, False)
            for k in range(2):
                give(other, k, c, other * 2 + k)
        if c + ahead < parts:
            send_tokens(c + ahead)

    def exchange(c):
        rows = rows_of(c)
        keeps[c].wait()
        for k in range(1, tp_count):
            source = (tp + k) % tp_count
            arrived(landed[c].at[source], land_sem.at[source, c], "tp", source)

        @pl.loop(0, seq_count)
        def _(j):
            kv_head = j * here // GROUP
            for k in range(2):
                sent[j, here + k, rows] = landed[c][
                    kv_head // kv_per, q_per + k * kv_per + kv_head % kv_per
                ]

        for j in near:
            send(
                sent.at[j, pl.ds(here, 2), rows], kv_ref.at[tp, seq, :, rows],
                kv_sem.at[seq, c], "seq", j,
            )
        hold(sent.at[seq, pl.ds(here, 2), rows], kv_ref.at[tp, seq, :, rows], hold_sem.at[0, c])

        @pl.loop(0, seq_count)
        def _(j):
            for k in range(here):
                head = index_ref[j * here + k]
                sent[j, k, rows] = landed[c][head // q_per, head % q_per]

        for j in near:
            send(
                sent.at[j, pl.ds(0, here), rows], q_ref.at[seq, :, rows],
                q_sem.at[seq, c], "seq", j,
            )
        hold(sent.at[seq, pl.ds(0, here), rows], q_ref.at[seq, :, rows], hold_sem.at[1, c])

    def spread(c):
        rows = rows_of(c)
        locals_[2 * c].wait()
        for source in near:
            arrived(kv_ref.at[tp, source, :, rows], kv_sem.at[source, c], "seq", source)
        block = kv_ref.at[tp, :, :, rows]
        for other in others:
            send(block, block, spread_sem.at[tp, c], "tp", other * 2 + core)
        send(block, block, spread_sem.at[tp, c], "tp", partner)

    def forward(c):
        for other in others:
            far = other * 2 + core
            block = kv_ref.at[far, :, :, rows_of(c)]
            arrived(block, spread_sem.at[far, c], "tp", far)
            send(block, block, spread_sem.at[far, c], "tp", partner)

    own_copy.wait()
    for c in range(parts):
        arrived(x_all.at[chip, 1 - core, rows_of(c)], x_sem.at[chip, 1 - core, c], "tp", partner)
    compute(chip, 0, own, True)
    keeps = [
        pltpu.make_async_copy(
            stage.at[chip, core, :, rows_of(c)], landed[c].at[tp], keep_sem.at[c]
        )
        for c in range(parts)
    ]
    for c in range(parts):
        keeps[c].start()
        give(chip, 1 - core, c, partner)

    for step in range(parts + 3):
        if step < parts:
            project(step)
        if 0 <= step - 1 < parts:
            exchange(step - 1)
        if 0 <= step - 2 < parts:
            spread(step - 2)
        if 0 <= step - 3 < parts:
            forward(step - 3)

    for c in range(parts):
        locals_[2 * c + 1].wait()
        for k in range(chips):
            source = (chip + k) % chips * 2 + 1 - core
            arrived(kv_ref.at[source, :, :, rows_of(c)], spread_sem.at[source, c], "tp", partner)

    block = tp_count * own
    rows = here * own
    factor = (DH**-0.5) * LOG2_E

    def toggled(change):
        result, bit = 0, 1
        while bit < seq_count:
            mine, flip = seq // bit % 2, change // bit % 2
            result = result + bit * (mine + flip - 2 * mine * flip)
            bit *= 2
        return result

    def attend(step):
        q = q_ref[step].reshape(rows, DH)
        docs = doc_ref[pl.ds(step * tp_count + tp, 1), :]
        docs = jnp.broadcast_to(docs, (own, own)).T[:, :1]
        docs = jnp.concatenate([docs] * here, 0)
        places = tp * own + lax.broadcasted_iota(jnp.int32, (own, 1), 0)
        places = jnp.concatenate([places] * here, 0)

        def body(index, carry, own_block=False):
            top, total, acc = carry
            keys = kv_ref[:, index, 0].reshape(block, DH)
            values = kv_ref[:, index, 1].reshape(block, DH)
            scores = lax.dot_general(
                q, keys, (((1,), (1,)), ((), ())), preferred_element_type=jnp.float32
            )
            key_docs = jnp.concatenate(
                [doc_ref[pl.ds(index * tp_count + c, 1), :] for c in range(tp_count)], 1
            )
            kept = key_docs == docs
            if own_block:
                kept = kept & (lax.broadcasted_iota(jnp.int32, (1, block), 1) <= places)
            scores = jnp.where(kept, scores, NEG_BIG)
            new_top = jnp.maximum(top, jnp.max(scores, 1, keepdims=True))
            shrink = jnp.exp2((top - new_top) * factor)
            powers = jnp.exp2((scores - new_top) * factor)
            total = total * shrink + jnp.sum(powers, 1, keepdims=True)
            acc = acc * shrink + jnp.dot(
                powers.astype(jnp.bfloat16), values, preferred_element_type=jnp.float32
            )
            return new_top, total, acc

        start = (
            jnp.full((rows, 1), NEG_BIG, jnp.float32),
            jnp.zeros((rows, 1), jnp.float32),
            jnp.zeros((rows, DH), jnp.float32),
        )
        _, total, acc = lax.fori_loop(0, step, body, body(step, start, True))
        return (acc / total).astype(jnp.bfloat16).reshape(here, own, DH)

    def outgoing(change):
        target = toggled(change)
        return target, pltpu.make_async_remote_copy(
            src_ref=context.at[change], dst_ref=final.at[seq], send_sem=give_sem.at[change],
            recv_sem=final_sem.at[seq], device_id={"seq": target}, device_id_type=MESH,
        )

    def hand(change):
        target, copy = outgoing(change)
        for c in range(parts):
            arrived(q_ref.at[target, :, rows_of(c)], q_sem.at[target, c], "seq", target)
        context[change] = attend(target)
        copy.start()

    half = seq_count // 2

    @pl.loop(0, half)
    def _(i):
        hand(half + i)

    @pl.loop(0, half - 1)
    def _(i):
        hand(half - 1 - i)

    final[seq] = attend(seq)

    @pl.loop(1, seq_count)
    def _(change):
        source = toggled(change)
        pltpu.make_async_remote_copy(
            src_ref=final.at[source], dst_ref=final.at[source], send_sem=give_sem.at[0],
            recv_sem=final_sem.at[source], device_id={"seq": source}, device_id_type=MESH,
        ).wait_recv()

    for head in range(seq_count * here):
        slot = slot_ref[head]
        out_ref[:, head * DH : (head + 1) * DH] = final[slot // here, slot % here]

    @pl.loop(1, seq_count)
    def _(change):
        outgoing(change)[1].wait_send()
    for copy in sends:
        copy.wait_send()


PARTS = 4
AHEAD = 2


def layer(
    index, slot, document_index, tokens, w, down, up, cosine, sine, tp_count, seq_count,
    rotated_heads,
):
    own, width = tokens.shape
    heads = w.shape[1] // DH
    pair = 2
    steps = heads // pair
    chips = tp_count // 2
    here = H // seq_count
    rank = down.shape[1]
    parts = PARTS
    vmem = pl.BlockSpec(memory_space=pltpu.VMEM)
    smem = pl.BlockSpec(memory_space=pltpu.SMEM)
    anywhere = pl.BlockSpec(memory_space=pl.ANY)
    count = 3 * parts * (2 * (chips - 1) + 1) + 2 * parts * (seq_count - 1)
    bf16 = jnp.bfloat16
    dma = pltpu.SemaphoreType.DMA
    mine = (seq_count, here, own, DH)
    return pl.pallas_call(
        functools.partial(layer_kernel, rotated_heads // pair, here, AHEAD),
        in_specs=[smem, smem, vmem, anywhere, anywhere, vmem, vmem, vmem, vmem],
        out_specs=vmem,
        out_shape=jax.ShapeDtypeStruct((own, H * DH), bf16),
        scratch_shapes=[
            pltpu.VMEM((chips, 2, own, width), bf16),
            pltpu.VMEM((steps, width, pair * DH), bf16),
            pltpu.VMEM((chips, 2, heads, own, DH), bf16),
            pltpu.VMEM((seq_count, here + 2, own, DH), bf16),
            pltpu.VMEM((2 * own, rank), bf16),
            pltpu.VMEM(mine, bf16),
            pltpu.VMEM((tp_count, seq_count, 2, own, DH), bf16),
            pltpu.VMEM(mine, bf16),
            pltpu.VMEM(mine, bf16),
            dma((steps,)),
            dma(()),
            dma((parts,)),
            dma((2, parts)),
            dma((count,)),
            dma((chips, 2, parts)),
            dma((tp_count, parts)),
            dma((seq_count, parts)),
            dma((seq_count, parts)),
            dma((tp_count, parts)),
            dma((seq_count,)),
            dma((seq_count,)),
        ]
        + [pltpu.VMEM((tp_count, heads, own // parts, DH), bf16)] * parts,
        compiler_params=pltpu.CompilerParams(collective_id=0, has_side_effects=True),
        name="layer",
    )(
        index, slot, document_index.reshape(-1, own), tokens, w, down.T, up, cosine, sine,
    )


def head_tables(query_to_key_head):
    heads = jnp.arange(H, dtype=jnp.int32)
    same = query_to_key_head[:, None] == query_to_key_head[None, :]
    earlier = heads[None, :] < heads[:, None]
    slot = GROUP * query_to_key_head + jnp.sum((same & earlier).astype(jnp.int32), 1)
    order = jnp.sum(jnp.where(slot[None, :] == heads[:, None], heads[None, :], 0), 1)
    return order.astype(jnp.int32), slot.astype(jnp.int32)


def per_device(
    tokens,
    joined_projection_weight,
    adapter_down_weight,
    adapter_up_weight,
    document_index,
    query_to_key_head,
):
    tp_count = lax.axis_size("tp")
    seq_count = lax.axis_size("seq")
    tp_rank = lax.axis_index("tp")
    seq_rank = lax.axis_index("seq")
    own = tokens.shape[0]
    block = own * tp_count
    here = H // seq_count
    q_per, kv_per = H // tp_count, KV // tp_count

    index, slot = head_tables(query_to_key_head)
    places = (seq_rank * block + jnp.arange(block, dtype=jnp.int32)).astype(jnp.float32)
    cosine, sine = rope_tables(places)
    table = (1, tp_count // 2, 2, own, DH)
    cosine = jnp.concatenate([cosine.reshape(table), jnp.ones(table, jnp.float32)])
    sine = jnp.concatenate([sine.reshape(table), jnp.zeros(table, jnp.float32)])
    return layer(
        index, slot, document_index, tokens, joined_projection_weight, adapter_down_weight,
        adapter_up_weight, cosine, sine, tp_count, seq_count, q_per + kv_per,
    )


def solution(mesh):
    return jax.shard_map(
        per_device,
        mesh=mesh,
        in_specs=(P(("seq", "tp"), None), P(None, "tp"), P(), P(None, "tp"), P(), P()),
        out_specs=P(("seq", "tp"), None),
        check_vma=False,
    )
```

```python
import functools

import jax
import jax.numpy as jnp
from jax import lax
from jax.experimental import pallas as pl
from jax.experimental.pallas import tpu as pltpu
from jax.sharding import PartitionSpec as P

H = 32
KV = 8
DH = 128
GROUP = H // KV

ADAPTER_SCALE = 0.5
THETA = 500000.0
NEG_BIG = -1e30
LOG2_E = 1.4426950408889634


MESH = pl.DeviceIdType.MESH


def layer_kernel(
    rotated, here, ahead, choice_ref, doc_ref, frequency_ref, tokens_ref, w_ref, down_ref, up_ref,
    out_ref,
    x_all, w_all, stage, sent, mid_ref, q_ref, kv_ref, context, final, cos_ref, sin_ref,
    tables, slot_ref, index_ref,
    w_sem, own_sem, keep_sem, hold_sem, send_sem, x_sem, land_sem, q_sem, kv_sem, spread_sem,
    give_sem, final_sem, kv_send_sem, table_sem, *landed,
):
    tp = lax.axis_index("tp")
    seq = lax.axis_index("seq")
    chips, _, own, width = x_all.shape
    parts, part = len(landed), landed[0].shape[2]
    tp_count, seq_count = 2 * chips, q_ref.shape[0]
    steps = w_all.shape[0]
    wide = w_all.shape[2]
    group = wide // DH
    chip, core = tp // 2, tp % 2
    partner = chip * 2 + (1 - core)
    others = [(chip + k) % chips for k in range(1, chips)]
    near = [(seq + k) % seq_count for k in range(1, seq_count)]
    q_per = H // tp_count
    kv_per = KV // tp_count
    sends = []
    locals_ = []

    def send(src, dst, sem, axis, target):
        copy = pltpu.make_async_remote_copy(
            src_ref=src, dst_ref=dst, send_sem=send_sem.at[len(sends)], recv_sem=sem,
            device_id={axis: target}, device_id_type=MESH,
        )
        copy.start()
        sends.append(copy)

    def arrived(dst, sem, axis, source):
        pltpu.make_async_remote_copy(
            src_ref=dst, dst_ref=dst, send_sem=send_sem.at[0], recv_sem=sem,
            device_id={axis: source}, device_id_type=MESH,
        ).wait_recv()

    def weight_copy(step):
        return pltpu.make_async_copy(
            w_ref.at[:, pl.ds(pl.multiple_of(step * wide, wide), wide)], w_all.at[step], w_sem.at[step]
        )

    def rows_of(c):
        return pl.ds(c * part, part)

    own_copy = pltpu.make_async_copy(tokens_ref, x_all.at[chip, core], own_sem)
    own_copy.start()
    for step in range(steps):
        weight_copy(step).start()

    barrier = pltpu.get_barrier_semaphore()
    for k in range(1, tp_count):
        pl.semaphore_signal(
            barrier, inc=1, device_id={"tp": (tp + k) % tp_count}, device_id_type=MESH
        )
    for k in range(1, seq_count):
        pl.semaphore_signal(
            barrier, inc=1, device_id={"seq": (seq + k) % seq_count}, device_id_type=MESH
        )
    pl.semaphore_wait(barrier, tp_count - 1 + seq_count - 1)

    def send_tokens(c):
        for other in others:
            send(
                tokens_ref.at[rows_of(c)], x_all.at[chip, core, rows_of(c)],
                x_sem.at[chip, core, c], "tp", other * 2 + core,
            )

    for c in range(min(ahead, parts)):
        send_tokens(c)
    for c in range(parts):
        send(
            tokens_ref.at[rows_of(c)], x_all.at[chip, core, rows_of(c)],
            x_sem.at[chip, core, c], "tp", partner,
        )

    def compute(c):
        rows = rows_of(c)
        count = 2 * chips * part
        mid_ref[...] = lax.dot_general(
            x_all[:, :, rows, :].reshape(count, width), down_ref[...], (((1,), (1,)), ((), ())),
            preferred_element_type=jnp.float32,
        ).astype(jnp.bfloat16)

        @pl.loop(0, steps)
        def _(step):
            if c == 0:
                weight_copy(step).wait()
            joined = jnp.dot(
                x_all[:, :, rows, :].reshape(count, width), w_all[step],
                preferred_element_type=jnp.float32,
            )
            joined = joined + ADAPTER_SCALE * jnp.dot(
                mid_ref[...], up_ref[:, pl.ds(pl.multiple_of(step * wide, wide), wide)],
                preferred_element_type=jnp.float32
            )
            for n in range(group):
                head = step * group + n
                kind = head // rotated
                cosine = cos_ref[kind, :, rows, :].reshape(count, DH)
                sine = sin_ref[kind, :, rows, :].reshape(count, DH)
                piece = joined[:, n * DH : (n + 1) * DH]
                piece = piece * cosine + pltpu.roll(piece, DH // 2, 1) * sine
                piece = piece.astype(jnp.bfloat16)
                for place in range(2 * chips):
                    stage[place // 2, place % 2, head, rows] = piece[
                        place * part : (place + 1) * part
                    ]

    def make_tables():
        for place in range(2 * chips):
            row = lax.broadcasted_iota(jnp.int32, (own, DH), 0)
            row = (seq * (2 * chips) + place) * own + row
            angles = row.astype(jnp.float32) * frequency_ref[...]
            sine = jnp.sin(angles)
            low = lax.broadcasted_iota(jnp.int32, (own, DH), 1) < DH // 2
            cos_ref[0, place] = jnp.cos(angles)
            sin_ref[0, place] = jnp.where(low, -sine, sine)
            cos_ref[1, place] = jnp.ones((own, DH), jnp.float32)
            sin_ref[1, place] = jnp.zeros((own, DH), jnp.float32)
        lane = lax.broadcasted_iota(jnp.int32, tables.shape, 1)
        choice = jnp.zeros(tables.shape, jnp.int32)
        for head in range(H):
            choice = jnp.where(lane == head, choice_ref[head], choice)
        slot = GROUP * choice
        for head in range(H):
            slot = slot + jnp.where((choice == choice_ref[head]) & (lane > head), 1, 0)
        tables[...] = slot
        copy = pltpu.make_async_copy(tables, slot_ref, table_sem)
        copy.start()
        copy.wait()
        order = jnp.zeros(tables.shape, jnp.int32)
        for head in range(H):
            order = order + jnp.where(lane == slot_ref[0, head], head, 0)
        tables[...] = order
        copy = pltpu.make_async_copy(tables, index_ref, table_sem)
        copy.start()
        copy.wait()

    def give(where, k, c, target):
        send(
            stage.at[where, k, :, rows_of(c)], landed[c].at[tp], land_sem.at[tp, c], "tp", target
        )

    def hold(src, dst, sem):
        copy = pltpu.make_async_copy(src, dst, sem)
        copy.start()
        locals_.append(copy)

    def relay(c):
        for other in others:
            block = x_all.at[other, core, rows_of(c)]
            arrived(block, x_sem.at[other, core, c], "tp", other * 2 + core)
            send(block, block, x_sem.at[other, core, c], "tp", partner)

    def project(c):
        for where in [chip] + others:
            arrived(
                x_all.at[where, 1 - core, rows_of(c)], x_sem.at[where, 1 - core, c], "tp", partner
            )
        compute(c)
        for other in others:
            for k in range(2):
                give(other, k, c, other * 2 + k)
        keeps[c].start()
        give(chip, 1 - core, c, partner)
        if c + ahead < parts:
            send_tokens(c + ahead)

    def home(j):
        return j * here // GROUP // kv_per // 2

    def fill(where, c):
        @pl.loop(0, seq_count // chips)
        def _(k):
            j = where * (seq_count // chips) + k
            kv_head = j * here // GROUP
            for n in range(2):
                sent[j, here + n, rows_of(c)] = landed[c][
                    kv_head // kv_per, q_per + n * kv_per + kv_head % kv_per
                ]

    def kv_send(c, k):
        j = near[k]
        return j, pltpu.make_async_remote_copy(
            src_ref=sent.at[j, pl.ds(here, 2), rows_of(c)],
            dst_ref=kv_ref.at[tp, seq, :, rows_of(c)],
            send_sem=kv_send_sem.at[c, k], recv_sem=kv_sem.at[seq, c],
            device_id={"seq": j}, device_id_type=MESH,
        )

    kv_sends = [[kv_send(c, k) for k in range(seq_count - 1)] for c in range(parts)]

    def early(c):
        keeps[c].wait()
        arrived(landed[c].at[partner], land_sem.at[partner, c], "tp", partner)
        fill(chip, c)
        for j, copy in kv_sends[c]:

            @pl.when(home(j) == chip)
            def _():
                copy.start()

    def exchange(c):
        rows = rows_of(c)
        for other in others:
            for k in range(2):
                source = other * 2 + k
                arrived(landed[c].at[source], land_sem.at[source, c], "tp", source)
            fill(other, c)
        for j, copy in kv_sends[c]:

            @pl.when(home(j) != chip)
            def _():
                copy.start()

        hold(sent.at[seq, pl.ds(here, 2), rows], kv_ref.at[tp, seq, :, rows], hold_sem.at[0, c])

        @pl.loop(0, seq_count)
        def _(j):
            for k in range(here):
                head = index_ref[0, j * here + k]
                sent[j, k, rows] = landed[c][head // q_per, head % q_per]

        for j in near:
            send(
                sent.at[j, pl.ds(0, here), rows], q_ref.at[seq, :, rows],
                q_sem.at[seq, c], "seq", j,
            )
        hold(sent.at[seq, pl.ds(0, here), rows], q_ref.at[seq, :, rows], hold_sem.at[1, c])

    def spread(c):
        rows = rows_of(c)
        locals_[2 * c].wait()
        for source in near:
            arrived(kv_ref.at[tp, source, :, rows], kv_sem.at[source, c], "seq", source)
        block = kv_ref.at[tp, :, :, rows]
        for other in others:
            send(block, block, spread_sem.at[tp, c], "tp", other * 2 + core)
        send(block, block, spread_sem.at[tp, c], "tp", partner)

    def forward(c):
        for other in others:
            far = other * 2 + core
            block = kv_ref.at[far, :, :, rows_of(c)]
            arrived(block, spread_sem.at[far, c], "tp", far)
            send(block, block, spread_sem.at[far, c], "tp", partner)

    make_tables()
    keeps = [
        pltpu.make_async_copy(
            stage.at[chip, core, :, rows_of(c)], landed[c].at[tp], keep_sem.at[c]
        )
        for c in range(parts)
    ]
    own_copy.wait()
    relay(0)
    for step in range(parts + 3):
        if step < parts:
            project(step)
            if step == 0 and parts > 1:
                relay(1)
            early(step)
        if 0 <= step - 1 < parts:
            exchange(step - 1)
        if 1 < step + 1 < parts:
            relay(step + 1)
        if 0 <= step - 2 < parts:
            spread(step - 2)
        if 0 <= step - 3 < parts:
            forward(step - 3)

    for c in range(parts):
        locals_[2 * c + 1].wait()
        for k in range(chips):
            source = (chip + k) % chips * 2 + 1 - core
            arrived(kv_ref.at[source, :, :, rows_of(c)], spread_sem.at[source, c], "tp", partner)

    block = tp_count * own
    rows = here * own
    factor = (DH**-0.5) * LOG2_E

    def toggled(change):
        result, bit = 0, 1
        while bit < seq_count:
            mine, flip = seq // bit % 2, change // bit % 2
            result = result + bit * (mine + flip - 2 * mine * flip)
            bit *= 2
        return result

    def attend(step):
        q = q_ref[step].reshape(rows, DH)
        docs = doc_ref[pl.ds(step * tp_count + tp, 1), :]
        docs = jnp.broadcast_to(docs, (own, own)).T[:, :1]
        docs = jnp.concatenate([docs] * here, 0)
        places = tp * own + lax.broadcasted_iota(jnp.int32, (own, 1), 0)
        places = jnp.concatenate([places] * here, 0)

        def body(index, carry, own_block=False):
            top, total, acc = carry
            keys = kv_ref[:, index, 0].reshape(block, DH)
            values = kv_ref[:, index, 1].reshape(block, DH)
            scores = lax.dot_general(
                q, keys, (((1,), (1,)), ((), ())), preferred_element_type=jnp.float32
            )
            key_docs = jnp.concatenate(
                [doc_ref[pl.ds(index * tp_count + c, 1), :] for c in range(tp_count)], 1
            )
            kept = key_docs == docs
            if own_block:
                kept = kept & (lax.broadcasted_iota(jnp.int32, (1, block), 1) <= places)
            scores = jnp.where(kept, scores, NEG_BIG)
            new_top = jnp.maximum(top, jnp.max(scores, 1, keepdims=True))
            shrink = jnp.exp2((top - new_top) * factor)
            powers = jnp.exp2((scores - new_top) * factor)
            total = total * shrink + jnp.sum(powers, 1, keepdims=True)
            acc = acc * shrink + jnp.dot(
                powers.astype(jnp.bfloat16), values, preferred_element_type=jnp.float32
            )
            return new_top, total, acc

        start = (
            jnp.full((rows, 1), NEG_BIG, jnp.float32),
            jnp.zeros((rows, 1), jnp.float32),
            jnp.zeros((rows, DH), jnp.float32),
        )
        _, total, acc = lax.fori_loop(0, step, body, body(step, start, True))
        return (acc / total).astype(jnp.bfloat16).reshape(here, own, DH)

    def outgoing(change):
        target = toggled(change)
        return target, pltpu.make_async_remote_copy(
            src_ref=context.at[change], dst_ref=final.at[seq], send_sem=give_sem.at[change],
            recv_sem=final_sem.at[seq], device_id={"seq": target}, device_id_type=MESH,
        )

    def hand(change):
        target, copy = outgoing(change)
        for c in range(parts):
            arrived(q_ref.at[target, :, rows_of(c)], q_sem.at[target, c], "seq", target)
        context[change] = attend(target)
        copy.start()

    half = seq_count // 2

    @pl.loop(0, half)
    def _(i):
        hand(half + i)

    @pl.loop(0, half - 1)
    def _(i):
        hand(half - 1 - i)

    final[seq] = attend(seq)

    @pl.loop(1, seq_count)
    def _(change):
        source = toggled(change)
        pltpu.make_async_remote_copy(
            src_ref=final.at[source], dst_ref=final.at[source], send_sem=give_sem.at[0],
            recv_sem=final_sem.at[source], device_id={"seq": source}, device_id_type=MESH,
        ).wait_recv()

    for head in range(seq_count * here):
        slot = slot_ref[0, head]
        out_ref[:, head * DH : (head + 1) * DH] = final[slot // here, slot % here]

    @pl.loop(1, seq_count)
    def _(change):
        outgoing(change)[1].wait_send()
    for copies in kv_sends:
        for _, copy in copies:
            copy.wait_send()
    for copy in sends:
        copy.wait_send()


PARTS = 4
AHEAD = 2
STEP_HEADS = 4


def layer(
    choice, document_index, tokens, w, down, up, frequency, tp_count, seq_count, rotated
):
    own, width = tokens.shape
    heads = w.shape[1] // DH
    group = STEP_HEADS
    steps = heads // group
    chips = tp_count // 2
    here = H // seq_count
    rank = down.shape[1]
    parts = PARTS
    vmem = pl.BlockSpec(memory_space=pltpu.VMEM)
    smem = pl.BlockSpec(memory_space=pltpu.SMEM)
    anywhere = pl.BlockSpec(memory_space=pl.ANY)
    count = 3 * parts * (2 * (chips - 1) + 1) + parts * (seq_count - 1)
    bf16, f32 = jnp.bfloat16, jnp.float32
    dma = pltpu.SemaphoreType.DMA
    mine = (seq_count, here, own, DH)
    return pl.pallas_call(
        functools.partial(layer_kernel, rotated, here, AHEAD),
        in_specs=[smem, vmem, vmem, anywhere, anywhere, vmem, vmem],
        out_specs=vmem,
        out_shape=jax.ShapeDtypeStruct((own, H * DH), bf16),
        scratch_shapes=[
            pltpu.VMEM((chips, 2, own, width), bf16),
            pltpu.VMEM((steps, width, group * DH), bf16),
            pltpu.VMEM((chips, 2, heads, own, DH), bf16),
            pltpu.VMEM((seq_count, here + 2, own, DH), bf16),
            pltpu.VMEM((tp_count * own // parts, rank), bf16),
            pltpu.VMEM(mine, bf16),
            pltpu.VMEM((tp_count, seq_count, 2, own, DH), bf16),
            pltpu.VMEM(mine, bf16),
            pltpu.VMEM(mine, bf16),
            pltpu.VMEM((2, tp_count, own, DH), f32),
            pltpu.VMEM((2, tp_count, own, DH), f32),
            pltpu.VMEM((8, 128), jnp.int32),
            pltpu.SMEM((8, 128), jnp.int32),
            pltpu.SMEM((8, 128), jnp.int32),
            dma((steps,)),
            dma(()),
            dma((parts,)),
            dma((2, parts)),
            dma((count,)),
            dma((chips, 2, parts)),
            dma((tp_count, parts)),
            dma((seq_count, parts)),
            dma((seq_count, parts)),
            dma((tp_count, parts)),
            dma((seq_count,)),
            dma((seq_count,)),
            dma((parts, seq_count - 1)),
            dma(()),
        ]
        + [pltpu.VMEM((tp_count, heads, own // parts, DH), bf16)] * parts,
        compiler_params=pltpu.CompilerParams(collective_id=0, has_side_effects=True),
        name="layer",
    )(choice, document_index.reshape(-1, own), frequency, tokens, w, down.T, up)


def per_device(
    tokens,
    joined_projection_weight,
    adapter_down_weight,
    adapter_up_weight,
    document_index,
    query_to_key_head,
):
    tp_count = lax.axis_size("tp")
    seq_count = lax.axis_size("seq")
    frequency = THETA ** (-(jnp.arange(DH // 2, dtype=jnp.float32) * 2.0) / DH)
    frequency = jnp.concatenate([frequency, frequency])[None, :]
    return layer(
        query_to_key_head, document_index, tokens, joined_projection_weight, adapter_down_weight,
        adapter_up_weight, frequency, tp_count, seq_count, (H + KV) // tp_count,
    )


def solution(mesh):
    return jax.shard_map(
        per_device,
        mesh=mesh,
        in_specs=(P(("seq", "tp"), None), P(None, "tp"), P(), P(None, "tp"), P(), P()),
        out_specs=P(("seq", "tp"), None),
        check_vma=False,
    )
```

```python
import functools

import jax
import jax.numpy as jnp
from jax import lax
from jax.experimental import pallas as pl
from jax.experimental.pallas import tpu as pltpu
from jax.sharding import PartitionSpec as P

H = 32
KV = 8
DH = 128
GROUP = H // KV

ADAPTER_SCALE = 0.5
THETA = 500000.0
NEG_BIG = -1e30
LOG2_E = 1.4426950408889634


MESH = pl.DeviceIdType.MESH


def layer_kernel(
    rotated, here, ahead, choice_ref, doc_ref, frequency_ref, tokens_ref, w_ref, down_ref, up_ref,
    out_ref,
    x_all, w_all, stage, sent, mid_ref, q_ref, kv_ref, context, final, cos_ref, sin_ref,
    tables, slot_ref, index_ref,
    landed_kv,
    w_sem, own_sem, keep_sem, hold_sem, send_sem, x_sem, land_sem, q_sem, kv_sem, spread_sem,
    give_sem, final_sem, kv_send_sem, table_sem, *landed,
):
    tp = lax.axis_index("tp")
    seq = lax.axis_index("seq")
    chips, _, own, width = x_all.shape
    parts, part = len(landed), landed[0].shape[2]
    tp_count, seq_count = 2 * chips, q_ref.shape[0]
    steps = w_all.shape[0]
    wide = w_all.shape[2]
    group = wide // DH
    chip, core = tp // 2, tp % 2
    partner = chip * 2 + (1 - core)
    others = [(chip + k) % chips for k in range(1, chips)]
    near = [(seq + k) % seq_count for k in range(1, seq_count)]
    q_per = H // tp_count
    kv_per = KV // tp_count
    sends = []
    q_steps = q_per // group

    def send(src, dst, sem, axis, target):
        copy = pltpu.make_async_remote_copy(
            src_ref=src, dst_ref=dst, send_sem=send_sem.at[len(sends)], recv_sem=sem,
            device_id={axis: target}, device_id_type=MESH,
        )
        copy.start()
        sends.append(copy)

    def arrived(dst, sem, axis, source):
        pltpu.make_async_remote_copy(
            src_ref=dst, dst_ref=dst, send_sem=send_sem.at[0], recv_sem=sem,
            device_id={axis: source}, device_id_type=MESH,
        ).wait_recv()

    def weight_copy(step):
        return pltpu.make_async_copy(
            w_ref.at[:, pl.ds(pl.multiple_of(step * wide, wide), wide)], w_all.at[step], w_sem.at[step]
        )

    def rows_of(c):
        return pl.ds(c * part, part)

    own_copy = pltpu.make_async_copy(tokens_ref, x_all.at[chip, core], own_sem)
    own_copy.start()
    for step in list(range(q_steps, steps)) + list(range(q_steps)):
        weight_copy(step).start()

    barrier = pltpu.get_barrier_semaphore()
    for k in range(1, tp_count):
        pl.semaphore_signal(
            barrier, inc=1, device_id={"tp": (tp + k) % tp_count}, device_id_type=MESH
        )
    for k in range(1, seq_count):
        pl.semaphore_signal(
            barrier, inc=1, device_id={"seq": (seq + k) % seq_count}, device_id_type=MESH
        )
    pl.semaphore_wait(barrier, tp_count - 1 + seq_count - 1)

    def send_tokens(c):
        for other in others:
            send(
                tokens_ref.at[rows_of(c)], x_all.at[chip, core, rows_of(c)],
                x_sem.at[chip, core, c], "tp", other * 2 + core,
            )

    for c in range(min(ahead, parts)):
        send_tokens(c)
    for c in range(parts):
        send(
            tokens_ref.at[rows_of(c)], x_all.at[chip, core, rows_of(c)],
            x_sem.at[chip, core, c], "tp", partner,
        )

    def compute(c, first, last):
        rows = rows_of(c)
        count = 2 * chips * part

        @pl.loop(first, last)
        def _(step):
            if c == 0:
                weight_copy(step).wait()
            joined = jnp.dot(
                x_all[:, :, rows, :].reshape(count, width), w_all[step],
                preferred_element_type=jnp.float32,
            )
            joined = joined + ADAPTER_SCALE * jnp.dot(
                mid_ref[c], up_ref[:, pl.ds(pl.multiple_of(step * wide, wide), wide)],
                preferred_element_type=jnp.float32
            )
            for n in range(group):
                head = step * group + n
                kind = head // rotated
                cosine = cos_ref[kind, :, rows, :].reshape(count, DH)
                sine = sin_ref[kind, :, rows, :].reshape(count, DH)
                piece = joined[:, n * DH : (n + 1) * DH]
                piece = piece * cosine + pltpu.roll(piece, DH // 2, 1) * sine
                piece = piece.astype(jnp.bfloat16)
                for place in range(2 * chips):
                    stage[place // 2, place % 2, head, rows] = piece[
                        place * part : (place + 1) * part
                    ]

    def make_tables():
        for place in range(2 * chips):
            row = lax.broadcasted_iota(jnp.int32, (own, DH), 0)
            row = (seq * (2 * chips) + place) * own + row
            angles = row.astype(jnp.float32) * frequency_ref[...]
            sine = jnp.sin(angles)
            low = lax.broadcasted_iota(jnp.int32, (own, DH), 1) < DH // 2
            cos_ref[0, place] = jnp.cos(angles)
            sin_ref[0, place] = jnp.where(low, -sine, sine)
            cos_ref[1, place] = jnp.ones((own, DH), jnp.float32)
            sin_ref[1, place] = jnp.zeros((own, DH), jnp.float32)
        lane = lax.broadcasted_iota(jnp.int32, tables.shape, 1)
        choice = jnp.zeros(tables.shape, jnp.int32)
        for head in range(H):
            choice = jnp.where(lane == head, choice_ref[head], choice)
        slot = GROUP * choice
        for head in range(H):
            slot = slot + jnp.where((choice == choice_ref[head]) & (lane > head), 1, 0)
        tables[...] = slot
        copy = pltpu.make_async_copy(tables, slot_ref, table_sem)
        copy.start()
        copy.wait()
        order = jnp.zeros(tables.shape, jnp.int32)
        for head in range(H):
            order = order + jnp.where(lane == slot_ref[0, head], head, 0)
        tables[...] = order
        copy = pltpu.make_async_copy(tables, index_ref, table_sem)
        copy.start()
        copy.wait()

    kv_heads, q_heads = pl.ds(q_per, 2 * kv_per), pl.ds(0, q_per)

    def keep(kind, c):
        heads, dst = ((kv_heads, landed_kv.at[c, tp]), (q_heads, landed[c].at[tp]))[kind]
        return pltpu.make_async_copy(
            stage.at[chip, core, heads, rows_of(c)], dst, keep_sem.at[kind, c]
        )

    def give(kind, c):
        heads, dst = ((kv_heads, landed_kv.at[c, tp]), (q_heads, landed[c].at[tp]))[kind]
        for other in others:
            for k in range(2):
                send(
                    stage.at[other, k, heads, rows_of(c)], dst, land_sem.at[kind, tp, c], "tp",
                    other * 2 + k,
                )
        keep(kind, c).start()
        send(
            stage.at[chip, 1 - core, heads, rows_of(c)], dst, land_sem.at[kind, tp, c], "tp",
            partner,
        )

    def relay(c):
        for other in others:
            block = x_all.at[other, core, rows_of(c)]
            arrived(block, x_sem.at[other, core, c], "tp", other * 2 + core)
            send(block, block, x_sem.at[other, core, c], "tp", partner)

    def project_kv(c):
        for where in [chip] + others:
            arrived(
                x_all.at[where, 1 - core, rows_of(c)], x_sem.at[where, 1 - core, c], "tp", partner
            )
        mid_ref[c] = lax.dot_general(
            x_all[:, :, rows_of(c), :].reshape(2 * chips * part, width), down_ref[...],
            (((1,), (1,)), ((), ())), preferred_element_type=jnp.float32,
        ).astype(jnp.bfloat16)
        compute(c, q_steps, steps)
        give(0, c)
        if c + ahead < parts:
            send_tokens(c + ahead)

    def project_q(c):
        compute(c, 0, q_steps)
        give(1, c)

    def home(j):
        return j * here // GROUP // kv_per // 2

    def fill(where, c):
        @pl.loop(0, seq_count // chips)
        def _(k):
            j = where * (seq_count // chips) + k
            kv_head = j * here // GROUP
            for n in range(2):
                sent[j, here + n, rows_of(c)] = landed_kv[
                    c, kv_head // kv_per, n * kv_per + kv_head % kv_per
                ]

    def kv_send(c, k):
        j = near[k]
        return j, pltpu.make_async_remote_copy(
            src_ref=sent.at[j, pl.ds(here, 2), rows_of(c)],
            dst_ref=kv_ref.at[tp, seq, :, rows_of(c)],
            send_sem=kv_send_sem.at[c, k], recv_sem=kv_sem.at[seq, c],
            device_id={"seq": j}, device_id_type=MESH,
        )

    kv_sends = [[kv_send(c, k) for k in range(seq_count - 1)] for c in range(parts)]

    def early(c):
        keep(0, c).wait()
        arrived(landed_kv.at[c, partner], land_sem.at[0, partner, c], "tp", partner)
        fill(chip, c)
        for j, copy in kv_sends[c]:

            @pl.when(home(j) == chip)
            def _():
                copy.start()

    def exchange_kv(c):
        for other in others:
            for k in range(2):
                source = other * 2 + k
                arrived(landed_kv.at[c, source], land_sem.at[0, source, c], "tp", source)
            fill(other, c)
        for j, copy in kv_sends[c]:

            @pl.when(home(j) != chip)
            def _():
                copy.start()

        hold_kv(c).start()

    def hold_kv(c):
        rows = rows_of(c)
        return pltpu.make_async_copy(
            sent.at[seq, pl.ds(here, 2), rows], kv_ref.at[tp, seq, :, rows], hold_sem.at[0, c]
        )

    def hold_q(c):
        rows = rows_of(c)
        return pltpu.make_async_copy(
            sent.at[seq, pl.ds(0, here), rows], q_ref.at[seq, :, rows], hold_sem.at[1, c]
        )

    def exchange_q(c):
        rows = rows_of(c)
        keep(1, c).wait()
        for k in range(1, tp_count):
            source = (tp + k) % tp_count
            arrived(landed[c].at[source], land_sem.at[1, source, c], "tp", source)

        @pl.loop(0, seq_count)
        def _(j):
            for k in range(here):
                head = index_ref[0, j * here + k]
                sent[j, k, rows] = landed[c][head // q_per, head % q_per]

        for j in near:
            send(
                sent.at[j, pl.ds(0, here), rows], q_ref.at[seq, :, rows],
                q_sem.at[seq, c], "seq", j,
            )
        hold_q(c).start()

    def spread(c):
        rows = rows_of(c)
        hold_kv(c).wait()
        for source in near:
            arrived(kv_ref.at[tp, source, :, rows], kv_sem.at[source, c], "seq", source)
        block = kv_ref.at[tp, :, :, rows]
        for other in others:
            send(block, block, spread_sem.at[tp, c], "tp", other * 2 + core)
        send(block, block, spread_sem.at[tp, c], "tp", partner)

    def forward(c):
        for other in others:
            far = other * 2 + core
            block = kv_ref.at[far, :, :, rows_of(c)]
            arrived(block, spread_sem.at[far, c], "tp", far)
            send(block, block, spread_sem.at[far, c], "tp", partner)

    make_tables()
    own_copy.wait()
    relay(0)
    for c in range(parts + 4):
        if c < parts:
            project_kv(c)
            if c == 0 and parts > 1:
                relay(1)
            early(c)
        if 0 <= c - 1 < parts:
            exchange_kv(c - 1)
        if 0 <= c - 2 < parts:
            project_q(c - 2)
        if 0 <= c - 3 < parts:
            spread(c - 3)
            exchange_q(c - 3)
        if 0 <= c - 4 < parts:
            forward(c - 4)
        if 1 < c + 1 < parts:
            relay(c + 1)

    for c in range(parts):
        hold_q(c).wait()
        for k in range(chips):
            source = (chip + k) % chips * 2 + 1 - core
            arrived(kv_ref.at[source, :, :, rows_of(c)], spread_sem.at[source, c], "tp", partner)

    block = tp_count * own
    slab = own // BANDS
    rows = here * slab
    factor = (DH**-0.5) * LOG2_E

    def toggled(change):
        result, bit = 0, 1
        while bit < seq_count:
            mine, flip = seq // bit % 2, change // bit % 2
            result = result + bit * (mine + flip - 2 * mine * flip)
            bit *= 2
        return result

    def band_of(band):
        return pl.ds(band * slab, slab)

    def attend(step, band):
        q = q_ref[step, :, band_of(band)].reshape(rows, DH)
        docs = doc_ref[pl.ds(step * tp_count + tp, 1), :]
        docs = jnp.broadcast_to(docs, (own, own)).T[band * slab : (band + 1) * slab, :1]
        docs = jnp.concatenate([docs] * here, 0)
        places = tp * own + band * slab + lax.broadcasted_iota(jnp.int32, (slab, 1), 0)
        places = jnp.concatenate([places] * here, 0)

        def body(index, carry, own_block=False):
            top, total, acc = carry
            keys = kv_ref[:, index, 0].reshape(block, DH)
            values = kv_ref[:, index, 1].reshape(block, DH)
            scores = lax.dot_general(
                q, keys, (((1,), (1,)), ((), ())), preferred_element_type=jnp.float32
            )
            key_docs = jnp.concatenate(
                [doc_ref[pl.ds(index * tp_count + c, 1), :] for c in range(tp_count)], 1
            )
            kept = key_docs == docs
            if own_block:
                kept = kept & (lax.broadcasted_iota(jnp.int32, (1, block), 1) <= places)
            scores = jnp.where(kept, scores, NEG_BIG)
            new_top = jnp.maximum(top, jnp.max(scores, 1, keepdims=True))
            shrink = jnp.exp2((top - new_top) * factor)
            powers = jnp.exp2((scores - new_top) * factor)
            total = total * shrink + jnp.sum(powers, 1, keepdims=True)
            acc = acc * shrink + jnp.dot(
                powers.astype(jnp.bfloat16), values, preferred_element_type=jnp.float32
            )
            return new_top, total, acc

        start = (
            jnp.full((rows, 1), NEG_BIG, jnp.float32),
            jnp.zeros((rows, 1), jnp.float32),
            jnp.zeros((rows, DH), jnp.float32),
        )
        _, total, acc = lax.fori_loop(0, step, body, body(step, start, True))
        return (acc / total).astype(jnp.bfloat16).reshape(here, slab, DH)

    def outgoing(change, band):
        target = toggled(change)
        return target, pltpu.make_async_remote_copy(
            src_ref=context.at[change, :, band_of(band)], dst_ref=final.at[seq, :, band_of(band)],
            send_sem=give_sem.at[change, band], recv_sem=final_sem.at[seq, band],
            device_id={"seq": target}, device_id_type=MESH,
        )

    def hand(change, band):
        target, copy = outgoing(change, band)
        for c in range(band * parts // BANDS, (band + 1) * parts // BANDS):
            arrived(q_ref.at[target, :, rows_of(c)], q_sem.at[target, c], "seq", target)
        context[change, :, band_of(band)] = attend(target, band)
        copy.start()

    half = seq_count // 2
    for band in range(BANDS):

        @pl.loop(0, half)
        def _(i):
            hand(half + i, band)

        @pl.loop(0, half - 1)
        def _(i):
            hand(half - 1 - i, band)

        final[seq, :, band_of(band)] = attend(seq, band)

    @pl.loop(1, seq_count)
    def _(change):
        source = toggled(change)
        for band in range(BANDS):
            dst = final.at[source, :, band_of(band)]
            pltpu.make_async_remote_copy(
                src_ref=dst, dst_ref=dst, send_sem=give_sem.at[0, 0],
                recv_sem=final_sem.at[source, band], device_id={"seq": source},
                device_id_type=MESH,
            ).wait_recv()

    for head in range(seq_count * here):
        slot = slot_ref[0, head]
        out_ref[:, head * DH : (head + 1) * DH] = final[slot // here, slot % here]

    @pl.loop(1, seq_count)
    def _(change):
        for band in range(BANDS):
            outgoing(change, band)[1].wait_send()
    for copies in kv_sends:
        for _, copy in copies:
            copy.wait_send()
    for copy in sends:
        copy.wait_send()


PARTS = 4
AHEAD = 2
STEP_HEADS = 4
BANDS = 1


def layer(
    choice, document_index, tokens, w, down, up, frequency, tp_count, seq_count, rotated
):
    own, width = tokens.shape
    heads = w.shape[1] // DH
    group = STEP_HEADS
    steps = heads // group
    chips = tp_count // 2
    here = H // seq_count
    rank = down.shape[1]
    parts = PARTS
    vmem = pl.BlockSpec(memory_space=pltpu.VMEM)
    smem = pl.BlockSpec(memory_space=pltpu.SMEM)
    anywhere = pl.BlockSpec(memory_space=pl.ANY)
    q_per = H // tp_count
    count = 4 * parts * (2 * (chips - 1) + 1) + parts * (seq_count - 1)
    bf16, f32 = jnp.bfloat16, jnp.float32
    dma = pltpu.SemaphoreType.DMA
    mine = (seq_count, here, own, DH)
    return pl.pallas_call(
        functools.partial(layer_kernel, rotated, here, AHEAD),
        in_specs=[smem, vmem, vmem, anywhere, anywhere, vmem, vmem],
        out_specs=vmem,
        out_shape=jax.ShapeDtypeStruct((own, H * DH), bf16),
        scratch_shapes=[
            pltpu.VMEM((chips, 2, own, width), bf16),
            pltpu.VMEM((steps, width, group * DH), bf16),
            pltpu.VMEM((chips, 2, heads, own, DH), bf16),
            pltpu.VMEM((seq_count, here + 2, own, DH), bf16),
            pltpu.VMEM((parts, tp_count * own // parts, rank), bf16),
            pltpu.VMEM(mine, bf16),
            pltpu.VMEM((tp_count, seq_count, 2, own, DH), bf16),
            pltpu.VMEM(mine, bf16),
            pltpu.VMEM(mine, bf16),
            pltpu.VMEM((2, tp_count, own, DH), f32),
            pltpu.VMEM((2, tp_count, own, DH), f32),
            pltpu.VMEM((8, 128), jnp.int32),
            pltpu.SMEM((8, 128), jnp.int32),
            pltpu.SMEM((8, 128), jnp.int32),
            pltpu.VMEM((parts, tp_count, heads - q_per, own // parts, DH), bf16),
            dma((steps,)),
            dma(()),
            dma((2, parts)),
            dma((2, parts)),
            dma((count,)),
            dma((chips, 2, parts)),
            dma((2, tp_count, parts)),
            dma((seq_count, parts)),
            dma((seq_count, parts)),
            dma((tp_count, parts)),
            dma((seq_count, BANDS)),
            dma((seq_count, BANDS)),
            dma((parts, seq_count - 1)),
            dma(()),
        ]
        + [pltpu.VMEM((tp_count, q_per, own // parts, DH), bf16)] * parts,
        compiler_params=pltpu.CompilerParams(collective_id=0, has_side_effects=True),
        name="layer",
    )(choice, document_index.reshape(-1, own), frequency, tokens, w, down.T, up)


def per_device(
    tokens,
    joined_projection_weight,
    adapter_down_weight,
    adapter_up_weight,
    document_index,
    query_to_key_head,
):
    tp_count = lax.axis_size("tp")
    seq_count = lax.axis_size("seq")
    frequency = THETA ** (-(jnp.arange(DH // 2, dtype=jnp.float32) * 2.0) / DH)
    frequency = jnp.concatenate([frequency, frequency])[None, :]
    return layer(
        query_to_key_head, document_index, tokens, joined_projection_weight, adapter_down_weight,
        adapter_up_weight, frequency, tp_count, seq_count, (H + KV) // tp_count,
    )


def solution(mesh):
    return jax.shard_map(
        per_device,
        mesh=mesh,
        in_specs=(P(("seq", "tp"), None), P(None, "tp"), P(), P(None, "tp"), P(), P()),
        out_specs=P(("seq", "tp"), None),
        check_vma=False,
    )
```
